32 devices in a mesh: tm: 4 (over z), space: 4 (over y, core), net: 2 (over x).
Axes of the slice: x: 2, y: 2, z: 4, core: 2. Of those that a mesh axis runs over, the one named last changes fastest.
Arguments:
- query_rows: bfloat16 [2, 4, 8, 64, 2560], P('net', 'tm', 'space'), may hold values from -140 to 140
- key_rows: bfloat16 [2, 4, 8, 64, 2560], P('net', 'tm', 'space'), may hold values from -8 to 8
- value_rows: bfloat16 [2, 4, 8, 64, 2560], P('net', 'tm', 'space'), may hold values from -6 to 6
- time_proj: bfloat16 [2, 256, 2560], P('net'), may hold values from -0.375 to 0.375
- block_list: int32 [4, 8, 9], P('tm', 'space'), may hold values from 0 to 31, as said below
- block_count: int32 [4, 8], P('tm', 'space'), may hold values from 1 to 9
- timestep: int32 [1], replicated, may hold values from 0 to 999
Outputs:
- latent_grad: bfloat16 [4, 8, 64, 2560], P('tm', 'space', None, 'net')
The draws below stay inside these ranges and needn't reach their ends.
Inputs may be any that keep to these rules, and one draw needn't show every extreme that they name: `block_list`: entry (f, b, s) names a block f2 * 8 + b2 with f2 within one of f and b2 within one of b, inside the grid; slot 0 is the query's own block; the first block_count[f, b] entries are distinct; the rest repeat the own block.
All inputs are finite; a program needn't handle non-finite values.
Results may differ from the reference program's by a relative error of at most 0.0053.
Values may be sent and summed in bfloat16 or wider, within the bound.
No kernel may reach another device: no remote copies, remote signals or barrier semaphores. Data moves between devices by JAX's collectives and lax.ppermute only.
A program may use at most 64 MiB of HBM per device.

```python
import jax
import jax.numpy as jnp
from jax import lax

HEADS = 20
HD = 128
FREQ = 256
BLK = 64
KSEL = 9
STEPS = 1000
HC = 2560
FRAMES = 4
SBLK = 8


def paired_fields(key):
    base = jax.random.fold_in(key, 41)
    query_key, key_key = jax.random.split(base, 2)
    shape = (2, FRAMES, SBLK, BLK, HEADS * HD)
    queries = jnp.clip(jax.random.normal(query_key, shape, jnp.float32), -6.0, 6.0)
    keyset = jnp.clip(jax.random.normal(key_key, shape, jnp.float32), -6.0, 6.0)
    return (queries, keyset)


def draw_query_rows(key, part):
    return paired_fields(key)[0].astype(jnp.bfloat16)


def draw_key_rows(key, part):
    return paired_fields(key)[1].astype(jnp.bfloat16)


def block_lists(key):
    base = jax.random.fold_in(key, 73)
    rank_key, dense_key, sparse_key = jax.random.split(base, 3)
    frame_step = jnp.array([-1, -1, -1, 0, 0, 1, 1, 1], jnp.int32)
    block_step = jnp.array([-1, 0, 1, -1, 1, -1, 0, 1], jnp.int32)
    frame = jnp.arange(FRAMES, dtype=jnp.int32)[:, None, None]
    block = jnp.arange(SBLK, dtype=jnp.int32)[None, :, None]
    near_frame = frame + frame_step
    near_block = block + block_step
    valid = (near_frame >= 0) & (near_frame < FRAMES) & (near_block >= 0) & (near_block < SBLK)
    ranks = jax.random.randint(rank_key, (FRAMES, SBLK, 8), 0, 1000) * 8 + jnp.arange(8, dtype=jnp.int32)
    ranks = ranks + (1 - valid.astype(jnp.int32)) * 100000
    order = jnp.argsort(ranks, axis=-1)
    chosen = jnp.take_along_axis(near_frame * SBLK + near_block, order, axis=-1)
    own = frame * SBLK + block
    lists = jnp.concatenate([own, chosen[:, :, :KSEL - 1]], axis=-1)
    live_count = jnp.sum(valid.astype(jnp.int32), axis=-1)
    middle = jnp.abs(frame[:, :, 0] - FRAMES // 2) <= FRAMES // 4
    dense = jax.random.randint(dense_key, (FRAMES, SBLK), KSEL - 3, KSEL + 1)
    sparse = jax.random.randint(sparse_key, (FRAMES, SBLK), 1, 4)
    count = jnp.minimum(jnp.where(middle, dense, sparse), 1 + live_count)
    count = count.at[1, 1].set(KSEL)
    slots = jnp.arange(KSEL, dtype=jnp.int32)
    lists = jnp.where(slots[None, None, :] < count[:, :, None], lists, own)
    return (lists.astype(jnp.int32), count.astype(jnp.int32))


def draw_block_list(key, part):
    return block_lists(key)[0]


def draw_block_count(key, part):
    return block_lists(key)[1]


def level_of(own_key, dims, cuts, smallest, top_value):
    level, own = 1.0, jax.random.fold_in(own_key, 6)
    for axis_at, shards_of in cuts:
        heights = jnp.exp(jax.random.uniform(jax.random.fold_in(own, axis_at), (shards_of,), jnp.float32, smallest / len(cuts), top_value / len(cuts)))
        level = level * jnp.repeat(heights, dims[axis_at] // shards_of).reshape([-1 if axis == axis_at else 1 for axis in range(len(dims))])
    return level


def centred(key, shape, width, bound, cuts=(), kind=jnp.bfloat16):
    entries = width * jax.random.normal(key, shape, jnp.float32)
    if cuts:
        entries = entries * level_of(key, shape, cuts, -0.22, 0.18)
    return jnp.clip(entries, -bound, bound).astype(kind)


def setup_inputs(seed: int = 0) -> dict:
    splits = jax.random.split(jax.random.key(seed), 8)
    query_rows = draw_query_rows(jax.random.fold_in(splits[7], 71), 0)
    key_rows = draw_key_rows(jax.random.fold_in(splits[7], 71), 0)
    value_rows = centred(splits[2], (2, FRAMES, SBLK, BLK, HC), 1.0, 6.0, ((0, 2), (1, 4), (2, 4)))
    time_proj = centred(splits[3], (2, FREQ, HC), FREQ ** -0.5, 0.375, ((0, 2),))
    block_list = draw_block_list(jax.random.fold_in(splits[7], 71), 0)
    block_count = draw_block_count(jax.random.fold_in(splits[7], 71), 0)
    timestep = jax.random.randint(splits[6], (1,), 0, STEPS).astype(jnp.int32)
    return dict(query_rows=query_rows, key_rows=key_rows, value_rows=value_rows, time_proj=time_proj, block_list=block_list, block_count=block_count, timestep=timestep)


def attend_network(query_net, key_net, value_net, block_list, block_count):
    key_flat = key_net.reshape(FRAMES * SBLK, BLK, HEADS, HD)
    value_flat = value_net.reshape(FRAMES * SBLK, BLK, HEADS, HD)
    scale = HD ** -0.5

    def one_frame(frame):
        queries = lax.dynamic_index_in_dim(query_net, frame, 0, keepdims=False)
        lists = lax.dynamic_index_in_dim(block_list, frame, 0, keepdims=False)
        counts = lax.dynamic_index_in_dim(block_count, frame, 0, keepdims=False)
        gathered_keys = key_flat[lists].reshape(SBLK, KSEL * BLK, HEADS, HD).astype(jnp.float32)
        gathered_values = value_flat[lists].reshape(SBLK, KSEL * BLK, HEADS, HD).astype(jnp.float32)
        query_heads = queries.reshape(SBLK, BLK, HEADS, HD).astype(jnp.float32)
        scores = jnp.einsum("qihd,qjhd->qhij", query_heads, gathered_keys) * scale
        slots = jnp.arange(KSEL, dtype=jnp.int32)
        live = jnp.repeat(slots[None, :] < counts[:, None], BLK, axis=1)
        scores = jnp.where(live[:, None, None, :], scores, jnp.float32(-1e30))
        top = jnp.max(scores, axis=-1, keepdims=True)
        expo = jnp.where(live[:, None, None, :], jnp.exp(scores - top), jnp.float32(0.0))
        total = jnp.sum(expo, axis=-1)
        weights = expo.astype(jnp.bfloat16).astype(jnp.float32)
        mixed = jnp.einsum("qhij,qjhd->qihd", weights, gathered_values)
        mixed = mixed / jnp.transpose(total, (0, 2, 1))[..., None]
        return mixed.reshape(SBLK, BLK, HEADS * HD)

    return lax.map(one_frame, jnp.arange(FRAMES, dtype=jnp.int32))


def gate_vector(timestep, proj):
    half = FREQ // 2
    freqs = jnp.exp(-jnp.log(jnp.float32(10000.0)) * jnp.arange(half, dtype=jnp.float32) / half)
    angle = timestep[0].astype(jnp.float32) * freqs
    feature = jax.nn.silu(jnp.concatenate([jnp.cos(angle), jnp.sin(angle)])).astype(jnp.bfloat16)
    return jnp.dot(feature[None, :], proj, preferred_element_type=jnp.float32)[0]


def reference(query_rows, key_rows, value_rows, time_proj, block_list, block_count, timestep):
    real_out = attend_network(query_rows[0], key_rows[0], value_rows[0], block_list, block_count)
    fake_out = attend_network(query_rows[1], key_rows[1], value_rows[1], block_list, block_count)
    real_gate = gate_vector(timestep, time_proj[0])
    fake_gate = gate_vector(timestep, time_proj[1])
    return (fake_gate * fake_out - real_gate * real_out).astype(jnp.bfloat16)
```

```python
import functools

import jax
import jax.numpy as jnp
from jax import lax
from jax.experimental import pallas as pl
from jax.experimental.pallas import tpu as pltpu
from jax.sharding import PartitionSpec as P

HD = 128
FREQ = 256
DEAD = -1e30


def swaps(count, first):
    pairs = [(i, i + 1) for i in range(first, count - 1, 2)]
    return pairs + [(b, a) for a, b in pairs]


def gate_vector(timestep, proj):
    half = FREQ // 2
    freqs = jnp.exp(-jnp.log(jnp.float32(10000.0)) * jnp.arange(half, dtype=jnp.float32) / half)
    angle = timestep[0].astype(jnp.float32) * freqs
    feature = jax.nn.silu(jnp.concatenate([jnp.cos(angle), jnp.sin(angle)])).astype(jnp.bfloat16)
    return jnp.dot(feature[None, :], proj, preferred_element_type=jnp.float32)


def attend(width, half_ref, bias_ref, gate_ref, q_ref, k_ref, v_ref, edge_ref, inner_ref,
           own_cross_ref, own_chip_ref, cross_ref, chip_ref, out_ref):
    base = half_ref[0] * width
    block_len = q_ref.shape[1]
    for head in range(width // HD):
        here = slice(head * HD, (head + 1) * HD)
        there = pl.ds(pl.multiple_of(base + head * HD, HD), HD)
        queries = jnp.concatenate([q_ref[0, :, there], q_ref[1, :, there]], axis=0)

        def rows(side, own_ref):
            parts = [own_ref[0, :, there], own_ref[1, :, there],
                     own_cross_ref[side, :, there], own_chip_ref[side, :, there]]
            for frame in range(2):
                parts += [edge_ref[frame][side, :, here], inner_ref[frame][side, :, here],
                          cross_ref[side, frame, :, here], chip_ref[side, frame, :, here]]
            return jnp.concatenate(parts, axis=0)

        scores = lax.dot_general(
            queries, rows(0, k_ref), (((1,), (1,)), ((), ())), preferred_element_type=jnp.float32
        )
        scores = scores * HD ** (-0.5)
        expo, total = [], []
        for block in range(2):
            part = scores[block * block_len:(block + 1) * block_len] + bias_ref[block:block + 1, :]
            part = jnp.exp(part - jnp.max(part, axis=-1, keepdims=True))
            expo.append(part.astype(jnp.bfloat16))
            total.append(jnp.sum(part, axis=-1, keepdims=True))
        mixed = jnp.dot(
            jnp.concatenate(expo, axis=0), rows(1, v_ref), preferred_element_type=jnp.float32
        )
        mixed = mixed / jnp.concatenate(total, axis=0) * gate_ref[0:1, here]
        out_ref[0, :, here] = mixed[:block_len]
        out_ref[1, :, here] = mixed[block_len:]


def attention(half, bias, gate, queries, keys, values, edges, inners, own_cross, own_chip, cross, chip):
    blocks, block_len, _ = queries.shape
    width = gate.shape[-1]
    vmem = pl.BlockSpec(memory_space=pltpu.VMEM)

    def kernel(*refs):
        (half_ref, bias_ref, gate_ref, q_ref, k_ref, v_ref, ea, eb, ia, ib,
         ox, oc, cross_ref, chip_ref, out_ref) = refs
        attend(width, half_ref, bias_ref, gate_ref, q_ref, k_ref, v_ref, (ea, eb), (ia, ib),
               ox, oc, cross_ref, chip_ref, out_ref)

    keys_seen = bias.shape[-1]
    flops = 4 * blocks * block_len * keys_seen * width
    return pl.pallas_call(
        kernel,
        out_shape=jax.ShapeDtypeStruct((blocks, block_len, width), jnp.float32),
        in_specs=[pl.BlockSpec(memory_space=pltpu.SMEM)] + [vmem] * 13,
        out_specs=vmem,
        cost_estimate=pl.CostEstimate(
            flops=flops, bytes_accessed=4 * keys_seen * width,
            transcendentals=blocks * block_len * keys_seen * width // HD,
        ),
    )(half, bias, gate, queries, keys, values, *edges, *inners, own_cross, own_chip, cross, chip)


def shards(query_rows, key_rows, value_rows, time_proj, block_list, block_count, timestep):
    queries, keys, values = query_rows[0, 0], key_rows[0, 0], value_rows[0, 0]
    blocks_here, block_len, features = queries.shape
    assert query_rows.shape[1] == 1 and blocks_here == 2
    width = features // lax.axis_size("net")
    frame, space, net = lax.axis_index("tm"), lax.axis_index("space"), lax.axis_index("net")
    frames, total_blocks = lax.axis_size("tm"), blocks_here * lax.axis_size("space")
    odd = space % 2
    time_pairs = [swaps(frames, first) for first in (0, 1)]
    chip_pairs, cross_pairs = (swaps(lax.axis_size("space"), first) for first in (0, 1))

    def piece(which, half):
        start = (which, 0, half * width)
        return jnp.stack([
            lax.dynamic_slice(x, start, (1, block_len, width))[0] for x in (keys, values)
        ])

    def whole(which):
        return jnp.stack([lax.dynamic_index_in_dim(x, which, 0, keepdims=False) for x in (keys, values)])

    other = 1 - net
    sent = jnp.stack([piece(odd, other), piece(1 - odd, other)], axis=1)
    first = [lax.ppermute(sent, "tm", pairs) for pairs in time_pairs]
    own_cross = lax.ppermute(whole(odd), "space", cross_pairs)
    own_chip = lax.ppermute(whole(1 - odd), "space", chip_pairs)
    edge_sent, inner_sent = piece(odd, net), piece(1 - odd, net)
    edges = [lax.ppermute(edge_sent, "tm", pairs) for pairs in time_pairs]
    inners = [lax.ppermute(inner_sent, "tm", pairs) for pairs in time_pairs]

    step = 1 - 2 * (frame % 2)
    side = 2 * odd - 1
    edge_at, inner_at = 2 * space + odd, 2 * space + 1 - odd
    cross_at, chip_at = edge_at + side, inner_at - side
    at_block = jnp.stack([2 * space, 2 * space + 1, cross_at, chip_at] + [edge_at, inner_at, cross_at, chip_at] * 2)
    at_frame = jnp.stack([frame] * 4 + [frame + step] * 4 + [frame - step] * 4)
    inside = (at_frame >= 0) & (at_frame < frames) & (at_block >= 0) & (at_block < total_blocks)
    name = jnp.where(inside, at_frame * total_blocks + at_block, -1)
    listed = block_list.reshape(blocks_here, -1)
    slots = jnp.arange(listed.shape[-1], dtype=jnp.int32)
    listed = jnp.where(slots[None, :] < block_count.reshape(blocks_here, 1), listed, -2)
    live = jnp.any(listed[:, None, :] == name[None, :, None], axis=-1)
    bias = jnp.repeat(jnp.where(live, jnp.float32(0.0), jnp.float32(DEAD)), block_len, axis=1)

    polarity = 2.0 * net.astype(jnp.float32) - 1.0
    gate = polarity * gate_vector(timestep, time_proj[0])

    def gate_half(half):
        return lax.dynamic_slice(gate, (0, half * width), (1, width))

    first_cross = lax.ppermute(jnp.stack([x[:, 0] for x in first], axis=1), "space", cross_pairs)
    first_chip = lax.ppermute(jnp.stack([x[:, 1] for x in first], axis=1), "space", chip_pairs)
    away = attention(
        other[None], bias, gate_half(other), queries, keys, values,
        [x[:, 0] for x in first], [x[:, 1] for x in first], own_cross, own_chip, first_cross, first_chip,
    )
    arrived = lax.ppermute(away, "net", swaps(lax.axis_size("net"), 0))
    cross = lax.ppermute(jnp.stack(edges, axis=1), "space", cross_pairs)
    chip = lax.ppermute(jnp.stack(inners, axis=1), "space", chip_pairs)
    kept = attention(
        net[None], bias, gate_half(net), queries, keys, values,
        edges, inners, own_cross, own_chip, cross, chip,
    )
    return (kept + arrived).astype(jnp.bfloat16)[None]


def solution(mesh):
    return jax.shard_map(
        shards,
        mesh=mesh,
        in_specs=(
            P("net", "tm", "space", None, None),
            P("net", "tm", "space", None, None),
            P("net", "tm", "space", None, None),
            P("net", None, None),
            P("tm", "space", None),
            P("tm", "space"),
            P(),
        ),
        out_specs=P("tm", "space", None, "net"),
        check_vma=False,
    )
```

```python
import jax
import jax.numpy as jnp
from jax import lax
from jax.experimental import pallas as pl
from jax.experimental.pallas import tpu as pltpu
from jax.sharding import PartitionSpec as P


HD = 128
FREQ = 256
DEAD = -1e30
VMEM_LIMIT = 20 << 20


def side_by_side(arrays):
    return jnp.stack(arrays, axis=1)


def swaps(count, first):
    pairs = [(i, i + 1) for i in range(first, count - 1, 2)]
    return pairs + [(b, a) for a, b in pairs]


def time_feature(timestep):
    half = FREQ // 2
    freqs = jnp.exp(-jnp.log(jnp.float32(10000.0)) * jnp.arange(half, dtype=jnp.float32) / half)
    angle = timestep[0].astype(jnp.float32) * freqs
    return jax.nn.silu(jnp.concatenate([jnp.cos(angle), jnp.sin(angle)])).astype(jnp.bfloat16)[None, :]


def attend(scalars_ref, live_ref, feature_ref, proj_ref, q_ref, k_ref, v_ref, own_cross_ref, own_chip_ref,
           frames, out_ref):
    width = out_ref.shape[-1]
    block_len = q_ref.shape[1]
    base, sign = scalars_ref[0], scalars_ref[1].astype(jnp.float32)
    feature = jnp.broadcast_to(feature_ref[...], (16, feature_ref.shape[-1]))
    lane = lax.broadcasted_iota(jnp.int32, (1, 2 * block_len), 1)
    dead = [
        jnp.where(jnp.where(lane < block_len, live_ref[2 * at], live_ref[2 * at + 1]) > 0, 0.0, DEAD)
        for at in range(4 * (1 + len(frames)))
    ]
    for head in range(width // HD):
        here = slice(head * HD, (head + 1) * HD)
        there = pl.ds(pl.multiple_of(base + head * HD, HD), HD)

        def rows(side, own_ref):
            parts = [own_ref[0, :, there], own_ref[1, :, there],
                     own_cross_ref[side, :, there], own_chip_ref[side, :, there]]
            for blocks in frames:
                parts += blocks(side, here)
            return jnp.concatenate(parts, axis=0)

        queries = jnp.concatenate([q_ref[0, :, there], q_ref[1, :, there]], axis=0)
        scores = lax.dot_general(
            rows(0, k_ref), queries, (((1,), (1,)), ((), ())), preferred_element_type=jnp.float32
        )
        scores = scores * HD ** (-0.5)
        scores = jnp.concatenate(
            [scores[at * block_len:(at + 1) * block_len] + row for at, row in enumerate(dead)], axis=0
        )
        expo = jnp.exp(scores - jnp.max(scores, axis=0, keepdims=True))
        total = jnp.sum(expo, axis=0, keepdims=True)
        mixed = lax.dot_general(
            expo.astype(jnp.bfloat16), rows(1, v_ref), (((0,), (0,)), ((), ())),
            preferred_element_type=jnp.float32,
        )
        total = jnp.transpose(jnp.broadcast_to(total, (8, 2 * block_len)))[:, 0:1]
        gate = sign * jnp.dot(feature, proj_ref[:, there], preferred_element_type=jnp.float32)[0:1]
        mixed = mixed / total * gate
        out_ref[0, :, here] = mixed[:block_len].astype(out_ref.dtype)
        out_ref[1, :, here] = mixed[block_len:].astype(out_ref.dtype)


def attention(kernel, operands, width, dtype, keys_seen):
    queries = operands[4]
    blocks, block_len, _ = queries.shape
    vmem, smem = (pl.BlockSpec(memory_space=space) for space in (pltpu.VMEM, pltpu.SMEM))
    return pl.pallas_call(
        kernel,
        out_shape=jax.ShapeDtypeStruct((blocks, block_len, width), dtype),
        in_specs=[smem, smem] + [vmem] * (len(operands) - 2),
        out_specs=vmem,
        cost_estimate=pl.CostEstimate(
            flops=4 * blocks * block_len * keys_seen * width,
            bytes_accessed=4 * keys_seen * width,
            transcendentals=blocks * block_len * keys_seen * width // HD,
        ),
        compiler_params=pltpu.CompilerParams(vmem_limit_bytes=VMEM_LIMIT),
    )(*operands)


def attend_away(scalars, live, feature, proj, q, k, v, own_cross, own_chip, even, odd, cross, chip, out):
    def frame(at, near):
        return lambda side, here: [near[side, 0, :, here], near[side, 1, :, here],
                                   cross[side, at, :, here], chip[side, at, :, here]]

    attend(scalars, live, feature, proj, q, k, v, own_cross, own_chip, (frame(0, even), frame(1, odd)), out)


def attend_kept(scalars, live, feature, proj, q, k, v, own_cross, own_chip,
                even_edge, odd_edge, even_inner, odd_inner, cross, chip, out):
    def frame(at, edge, inner):
        return lambda side, here: [edge[side, :, here], inner[side, :, here],
                                   cross[side, at, :, here], chip[side, at, :, here]]

    frames = (frame(0, even_edge, even_inner), frame(1, odd_edge, odd_inner))
    attend(scalars, live, feature, proj, q, k, v, own_cross, own_chip, frames, out)


def shards(query_rows, key_rows, value_rows, time_proj, block_list, block_count, timestep):
    queries, keys, values = query_rows[0, 0], key_rows[0, 0], value_rows[0, 0]
    blocks_here, block_len, features = queries.shape
    assert query_rows.shape[1] == 1 and blocks_here == 2
    width = features // lax.axis_size("net")
    frame, space, net = lax.axis_index("tm"), lax.axis_index("space"), lax.axis_index("net")
    frames, total_blocks = lax.axis_size("tm"), blocks_here * lax.axis_size("space")
    odd = space % 2
    time_pairs = {"even": swaps(frames, 0), "odd": swaps(frames, 1)}
    chip_pairs, cross_pairs = (swaps(lax.axis_size("space"), first) for first in (0, 1))

    def piece(which, half):
        start = (which, 0, half * width)
        return jnp.stack([
            lax.dynamic_slice(x, start, (1, block_len, width))[0] for x in (keys, values)
        ])

    def whole(which):
        return jnp.stack([lax.dynamic_index_in_dim(x, which, 0, keepdims=False) for x in (keys, values)])

    other = 1 - net
    sent = jnp.stack([piece(odd, other), piece(1 - odd, other)], axis=1)
    first = [lax.ppermute(sent, "tm", time_pairs[turn]) for turn in time_pairs]
    own_cross = lax.ppermute(whole(odd), "space", cross_pairs)
    own_chip = lax.ppermute(whole(1 - odd), "space", chip_pairs)
    edge_sent, inner_sent = piece(odd, net), piece(1 - odd, net)
    edges = [lax.ppermute(edge_sent, "tm", time_pairs[turn]) for turn in time_pairs]
    inners = [lax.ppermute(inner_sent, "tm", time_pairs[turn]) for turn in time_pairs]

    step = 1 - 2 * (frame % 2)
    side = 2 * odd - 1
    edge_at, inner_at = 2 * space + odd, 2 * space + 1 - odd
    cross_at, chip_at = edge_at + side, inner_at - side
    at_block = jnp.stack([2 * space, 2 * space + 1, cross_at, chip_at] + [edge_at, inner_at, cross_at, chip_at] * 2)
    at_frame = jnp.stack([frame] * 4 + [frame + step] * 4 + [frame - step] * 4)
    inside = (at_frame >= 0) & (at_frame < frames) & (at_block >= 0) & (at_block < total_blocks)
    name = jnp.where(inside, at_frame * total_blocks + at_block, -1)
    listed = block_list.reshape(blocks_here, -1)
    slots = jnp.arange(listed.shape[-1], dtype=jnp.int32)
    listed = jnp.where(slots[None, :] < block_count.reshape(blocks_here, 1), listed, -2)
    live = jnp.any(listed[None, :, :] == name[:, None, None], axis=-1).astype(jnp.int32).reshape(-1)

    feature, proj = time_feature(timestep), time_proj[0]
    sign = 2 * net - 1
    shared = (feature, proj, queries, keys, values, own_cross, own_chip)
    keys_seen = name.shape[0] * block_len

    first_cross = lax.ppermute(jnp.stack([x[:, 0] for x in first], axis=1), "space", cross_pairs)
    first_chip = lax.ppermute(jnp.stack([x[:, 1] for x in first], axis=1), "space", chip_pairs)
    away = attention(
        attend_away, (jnp.stack([other * width, sign]), live, *shared, *first, first_cross, first_chip),
        width, jnp.bfloat16, keys_seen,
    )
    arrived = lax.ppermute(away, "net", swaps(lax.axis_size("net"), 0))
    cross = lax.ppermute(side_by_side(edges), "space", cross_pairs)
    chip = lax.ppermute(side_by_side(inners), "space", chip_pairs)
    kept = attention(
        attend_kept, (jnp.stack([net * width, sign]), live, *shared, *edges, *inners, cross, chip),
        width, jnp.float32, keys_seen,
    )
    return (kept + arrived).astype(jnp.bfloat16)[None]


def solution(mesh):
    return jax.shard_map(
        shards,
        mesh=mesh,
        in_specs=(
            P("net", "tm", "space", None, None),
            P("net", "tm", "space", None, None),
            P("net", "tm", "space", None, None),
            P("net", None, None),
            P("tm", "space", None),
            P("tm", "space"),
            P(),
        ),
        out_specs=P("tm", "space", None, "net"),
        check_vma=False,
    )
```

```python
import jax
import jax.numpy as jnp
from jax import lax
from jax.experimental import pallas as pl
from jax.experimental.pallas import tpu as pltpu
from jax.sharding import PartitionSpec as P


HD = 128
FREQ = 256
DEAD = -1e30
LOG2E = 1.4426950408889634
VMEM_LIMIT = 6 << 20
SMALL_LIMIT = 2 << 20


def swaps(count, first):
    pairs = [(i, i + 1) for i in range(first, count - 1, 2)]
    return pairs + [(b, a) for a, b in pairs]


def kernel_call(kernel, specs, out_shape, operands, **more):
    return pl.pallas_call(
        kernel, out_shape=out_shape, in_specs=specs,
        out_specs=jax.tree.map(lambda _: pl.BlockSpec(memory_space=pltpu.VMEM), out_shape),
        **more,
    )(*operands)


def on_chip(*arrays):
    return [pltpu.with_memory_space_constraint(x, pltpu.VMEM) for x in arrays]


def pack(at, keys, values, pieces):
    block_len = keys.shape[1]

    def kernel(at_ref, k_ref, v_ref, *rest):
        outs, sems = rest[:len(pieces)], rest[len(pieces)]
        copies = []
        for n, (block, first, width) in enumerate(pieces):
            start = 0 if first is None else pl.multiple_of(at_ref[first], HD)
            for side, source in enumerate((k_ref, v_ref)):
                copies.append(pltpu.make_async_copy(
                    source.at[at_ref[block], :, pl.ds(start, width)], outs[n].at[side], sems.at[n, side]
                ))
        for copy in copies:
            copy.start()
        for copy in copies:
            copy.wait()

    anywhere = pl.BlockSpec(memory_space=pltpu.HBM)
    return kernel_call(
        kernel, [pl.BlockSpec(memory_space=pltpu.SMEM), anywhere, anywhere],
        [jax.ShapeDtypeStruct((2, block_len, width), keys.dtype) for _, _, width in pieces],
        (at, keys, values),
        scratch_shapes=[pltpu.SemaphoreType.DMA((len(pieces), 2))],
        compiler_params=pltpu.CompilerParams(vmem_limit_bytes=SMALL_LIMIT),
    )


def join(even, odd):
    def kernel(even_ref, odd_ref, out_ref):
        out_ref[0] = even_ref[...]
        out_ref[1] = odd_ref[...]

    vmem = pl.BlockSpec(memory_space=pltpu.VMEM)
    return kernel_call(
        kernel, [vmem, vmem], jax.ShapeDtypeStruct((2, *even.shape), even.dtype), on_chip(even, odd),
        compiler_params=pltpu.CompilerParams(vmem_limit_bytes=SMALL_LIMIT),
    )


def time_feature(timestep):
    half = FREQ // 2
    freqs = jnp.exp(-jnp.log(jnp.float32(10000.0)) * jnp.arange(half, dtype=jnp.float32) / half)
    angle = timestep[0].astype(jnp.float32) * freqs
    return jax.nn.silu(jnp.concatenate([jnp.cos(angle), jnp.sin(angle)])).astype(jnp.bfloat16)[None, :]


def signed_gate(feature, proj, sign):
    def kernel(sign_ref, feature_ref, proj_ref, out_ref):
        rows = jnp.broadcast_to(feature_ref[...], (16, feature_ref.shape[-1]))
        gate = jnp.dot(rows, proj_ref[...], preferred_element_type=jnp.float32)
        out_ref[...] = gate[0:1] * sign_ref[0].astype(jnp.float32)

    vmem = pl.BlockSpec(memory_space=pltpu.VMEM)
    return kernel_call(
        kernel, [pl.BlockSpec(memory_space=pltpu.SMEM), vmem, vmem],
        jax.ShapeDtypeStruct((1, proj.shape[-1]), jnp.float32), (sign, feature, proj),
        compiler_params=pltpu.CompilerParams(vmem_limit_bytes=SMALL_LIMIT),
    )


def attend(first_ref, live_ref, gate_ref, q_ref, k_ref, v_ref, own_cross_ref, own_chip_ref,
           even_edge_ref, odd_edge_ref, even_inner_ref, odd_inner_ref, cross_ref, chip_ref, out_ref):
    heads = out_ref.shape[-1] // HD
    block_len = q_ref.shape[1]
    base = first_ref[0]
    near = ((even_edge_ref, even_inner_ref), (odd_edge_ref, odd_inner_ref))
    lane = lax.broadcasted_iota(jnp.int32, (1, 2 * block_len), 1)
    dead = [
        jnp.where(jnp.where(lane < block_len, live_ref[2 * at], live_ref[2 * at + 1]) > 0, 0.0, DEAD)
        for at in range(4 * (1 + len(near)))
    ]

    def at_head(head):
        return slice(head * HD, (head + 1) * HD), pl.ds(pl.multiple_of(base + head * HD, HD), HD)

    def rows(head, side, own_ref):
        here, there = at_head(head)
        parts = [own_ref[0, :, there], own_ref[1, :, there],
                 own_cross_ref[side, :, there], own_chip_ref[side, :, there]]
        for at, (edge_ref, inner_ref) in enumerate(near):
            parts += [edge_ref[side, :, here], inner_ref[side, :, here],
                      cross_ref[at, side, :, here], chip_ref[at, side, :, here]]
        return jnp.concatenate(parts, axis=0)

    def score(head):
        _, there = at_head(head)
        queries = jnp.concatenate([q_ref[0, :, there], q_ref[1, :, there]], axis=0)
        return lax.dot_general(
            rows(head, 0, k_ref), queries, (((1,), (1,)), ((), ())), preferred_element_type=jnp.float32
        )

    scores = score(0)
    for head in range(heads):
        here, there = at_head(head)
        later = score(head + 1) if head + 1 < heads else None
        scores = scores * (HD ** (-0.5) * LOG2E)
        scores = jnp.concatenate(
            [scores[at * block_len:(at + 1) * block_len] + row for at, row in enumerate(dead)], axis=0
        )
        expo = jnp.exp2(scores - jnp.max(scores, axis=0, keepdims=True))
        total = jnp.sum(expo, axis=0, keepdims=True)
        mixed = lax.dot_general(
            expo.astype(jnp.bfloat16), rows(head, 1, v_ref), (((0,), (0,)), ((), ())),
            preferred_element_type=jnp.float32,
        )
        total = jnp.transpose(jnp.broadcast_to(total, (8, 2 * block_len)))[:, 0:1]
        mixed = mixed / total * gate_ref[0:1, there]
        out_ref[0, :, here] = mixed[:block_len].astype(out_ref.dtype)
        out_ref[1, :, here] = mixed[block_len:].astype(out_ref.dtype)
        scores = later


def attention(first, live, operands, width, dtype):
    queries = operands[1]
    blocks, block_len, _ = queries.shape
    keys_seen = live.shape[0] // blocks * block_len
    vmem, smem = (pl.BlockSpec(memory_space=space) for space in (pltpu.VMEM, pltpu.SMEM))
    return kernel_call(
        attend, [smem, smem] + [vmem] * len(operands),
        jax.ShapeDtypeStruct((blocks, block_len, width), dtype),
        (first, live, *on_chip(*operands)),
        cost_estimate=pl.CostEstimate(
            flops=4 * blocks * block_len * keys_seen * width,
            bytes_accessed=4 * keys_seen * width,
            transcendentals=blocks * block_len * keys_seen * width // HD,
        ),
        compiler_params=pltpu.CompilerParams(vmem_limit_bytes=VMEM_LIMIT),
    )


def shards(query_rows, key_rows, value_rows, time_proj, block_list, block_count, timestep):
    queries, keys, values = query_rows[0, 0], key_rows[0, 0], value_rows[0, 0]
    blocks_here, _, features = queries.shape
    assert query_rows.shape[1] == 1 and blocks_here == 2
    width = features // lax.axis_size("net")
    frame, space, net = lax.axis_index("tm"), lax.axis_index("space"), lax.axis_index("net")
    frames, total_blocks = lax.axis_size("tm"), blocks_here * lax.axis_size("space")
    odd = space % 2
    time_pairs = (swaps(frames, 0), swaps(frames, 1))
    chip_pairs, cross_pairs = (swaps(lax.axis_size("space"), first) for first in (0, 1))
    away, kept = (1 - net) * width, net * width
    at = jnp.stack([odd, 1 - odd, away, kept])

    edge_away, inner_away = pack(at, keys, values, [(0, 2, width), (1, 2, width)])
    first_edge = [lax.ppermute(edge_away, "tm", pairs) for pairs in time_pairs]
    first_inner = [lax.ppermute(inner_away, "tm", pairs) for pairs in time_pairs]
    edge_own, inner_own, edge_kept, inner_kept = pack(
        at, keys, values, [(0, None, features), (1, None, features), (0, 3, width), (1, 3, width)]
    )
    own_cross = lax.ppermute(edge_own, "space", cross_pairs)
    own_chip = lax.ppermute(inner_own, "space", chip_pairs)
    kept_edge = [lax.ppermute(edge_kept, "tm", pairs) for pairs in time_pairs]
    kept_inner = [lax.ppermute(inner_kept, "tm", pairs) for pairs in time_pairs]

    step = 1 - 2 * (frame % 2)
    side = 2 * odd - 1
    edge_at, inner_at = 2 * space + odd, 2 * space + 1 - odd
    cross_at, chip_at = edge_at + side, inner_at - side
    at_block = jnp.stack([2 * space, 2 * space + 1, cross_at, chip_at] + [edge_at, inner_at, cross_at, chip_at] * 2)
    at_frame = jnp.stack([frame] * 4 + [frame + step] * 4 + [frame - step] * 4)
    inside = (at_frame >= 0) & (at_frame < frames) & (at_block >= 0) & (at_block < total_blocks)
    name = jnp.where(inside, at_frame * total_blocks + at_block, -1)
    listed = block_list.reshape(blocks_here, -1)
    slots = jnp.arange(listed.shape[-1], dtype=jnp.int32)
    listed = jnp.where(slots[None, :] < block_count.reshape(blocks_here, 1), listed, -2)
    live = jnp.any(listed[None, :, :] == name[:, None, None], axis=-1).astype(jnp.int32).reshape(-1)

    gate = signed_gate(time_feature(timestep), time_proj[0], (2 * net - 1)[None])
    shared = (gate, queries, keys, values, own_cross, own_chip)

    first_cross = lax.ppermute(join(*first_edge), "space", cross_pairs)
    first_chip = lax.ppermute(join(*first_inner), "space", chip_pairs)
    sent = attention(
        away[None], live, (*shared, *first_edge, *first_inner, first_cross, first_chip),
        width, jnp.bfloat16,
    )
    arrived = lax.ppermute(sent, "net", swaps(lax.axis_size("net"), 0))
    kept_cross = lax.ppermute(join(*kept_edge), "space", cross_pairs)
    kept_chip = lax.ppermute(join(*kept_inner), "space", chip_pairs)
    here = attention(
        kept[None], live, (*shared, *kept_edge, *kept_inner, kept_cross, kept_chip),
        width, jnp.float32,
    )
    return (here + arrived).astype(jnp.bfloat16)[None]


def solution(mesh):
    return jax.shard_map(
        shards,
        mesh=mesh,
        in_specs=(
            P("net", "tm", "space", None, None),
            P("net", "tm", "space", None, None),
            P("net", "tm", "space", None, None),
            P("net", None, None),
            P("tm", "space", None),
            P("tm", "space"),
            P(),
        ),
        out_specs=P("tm", "space", None, "net"),
        check_vma=False,
    )
```

```python
import functools

import jax
import jax.numpy as jnp
from jax import lax
from jax.experimental import pallas as pl
from jax.experimental.pallas import tpu as pltpu
from jax.sharding import PartitionSpec as P


HD = 128
FREQ = 256
DEAD = -1e30
LOG2E = 1.4426950408889634
VMEM_LIMIT = 6 << 20
SMALL_LIMIT = 2 << 20


def swaps(count, first):
    pairs = [(i, i + 1) for i in range(first, count - 1, 2)]
    return pairs + [(b, a) for a, b in pairs]


def kernel_call(kernel, specs, out_shape, operands, **more):
    return pl.pallas_call(
        kernel, out_shape=out_shape, in_specs=specs,
        out_specs=(
            [pl.BlockSpec(memory_space=pltpu.VMEM)] * len(out_shape) if isinstance(out_shape, list)
            else pl.BlockSpec(memory_space=pltpu.VMEM)
        ),
        **more,
    )(*operands)


def on_chip(*arrays):
    return [pltpu.with_memory_space_constraint(x, pltpu.VMEM) for x in arrays]


def place():
    odd = lax.rem(lax.axis_index("space"), 2)
    return odd, lax.axis_index("net")


def pack(keys, values, pieces, *gate_of):
    block_len, features = keys.shape[1:]
    half = features // lax.axis_size("net")
    widths = [features if which == "both" else half for _, which in pieces]

    def kernel(k_ref, v_ref, *rest):
        inputs, rest = rest[:len(gate_of)], rest[len(gate_of):]
        outs, rest = rest[:len(pieces)], rest[len(pieces):]
        odd, net = place()
        sems = rest[-1]
        copies = []
        for n, (block, which) in enumerate(pieces):
            row = odd if block == "edge" else 1 - odd
            start = {"both": 0, "kept": net * half, "away": (1 - net) * half}[which]
            if which != "both":
                start = pl.multiple_of(start, HD)
            for side, source in enumerate((k_ref, v_ref)):
                copies.append(pltpu.make_async_copy(
                    source.at[row, :, pl.ds(start, widths[n])], outs[n].at[side], sems.at[n, side]
                ))
        for copy in copies:
            copy.start()
        if gate_of:
            (feature_ref, proj_ref), (gate_ref, held_ref) = inputs, rest[:2]
            fetch = pltpu.make_async_copy(proj_ref, held_ref, sems.at[len(pieces), 0])
            fetch.start()
            fetch.wait()
            rows = jnp.broadcast_to(feature_ref[...], (16, feature_ref.shape[-1]))
            gate = jnp.dot(rows, held_ref[...], preferred_element_type=jnp.float32)
            gate_ref[...] = gate[0:1] * (2 * net - 1).astype(jnp.float32)
        for copy in copies:
            copy.wait()

    hbm, vmem = pl.BlockSpec(memory_space=pltpu.HBM), pl.BlockSpec(memory_space=pltpu.VMEM)
    operands = [pltpu.with_memory_space_constraint(x, pltpu.HBM) for x in (keys, values)]
    out_shape = [jax.ShapeDtypeStruct((2, block_len, width), keys.dtype) for width in widths]
    specs, scratch = [hbm, hbm], []
    if gate_of:
        feature, proj = gate_of
        operands += [feature, pltpu.with_memory_space_constraint(proj, pltpu.HBM)]
        specs += [vmem, hbm]
        out_shape.append(jax.ShapeDtypeStruct((1, features), jnp.float32))
        scratch = [pltpu.VMEM(proj.shape, proj.dtype)]
    return kernel_call(
        kernel, specs, out_shape, operands,
        scratch_shapes=[*scratch, pltpu.SemaphoreType.DMA((len(pieces) + 1, 2))],
        compiler_params=pltpu.CompilerParams(vmem_limit_bytes=VMEM_LIMIT),
    )


def join(odd, even):
    def kernel(even_ref, odd_ref, out_ref):
        out_ref[0] = even_ref[...]
        out_ref[1] = odd_ref[...]

    vmem = pl.BlockSpec(memory_space=pltpu.VMEM)
    return kernel_call(
        kernel, [vmem, vmem], jax.ShapeDtypeStruct((2, *even.shape), even.dtype), on_chip(even, odd),
        compiler_params=pltpu.CompilerParams(vmem_limit_bytes=SMALL_LIMIT),
    )


def time_feature(timestep):
    half = FREQ // 2
    freqs = jnp.exp(-jnp.log(jnp.float32(10000.0)) * jnp.arange(half, dtype=jnp.float32) / half)
    angle = timestep[0].astype(jnp.float32) * freqs
    return jax.nn.silu(jnp.concatenate([jnp.cos(angle), jnp.sin(angle)])).astype(jnp.bfloat16)[None, :]


def dead_rows(list_ref, count_ref, block_len):
    frame, space = lax.axis_index("tm"), lax.axis_index("space")
    frames, total_blocks = lax.axis_size("tm"), 2 * lax.axis_size("space")
    odd = lax.rem(space, 2)
    step, side = 1 - 2 * lax.rem(frame, 2), 2 * odd - 1
    edge_at, inner_at = 2 * space + odd, 2 * space + 1 - odd
    outer = [edge_at + side, inner_at - side]
    lane = lax.broadcasted_iota(jnp.int32, (1, 2 * block_len), 1)
    listed = [
        jnp.where(
            lane < block_len,
            jnp.where(slot < count_ref[0, 0], list_ref[0, slot], -2),
            jnp.where(slot < count_ref[0, 1], list_ref[1, slot], -2),
        )
        for slot in range(list_ref.shape[1])
    ]
    dead = []
    for at_frame, near in (
        (frame, [2 * space, 2 * space + 1]), (frame + step, [edge_at, inner_at]), (frame - step, [edge_at, inner_at]),
    ):
        for at_block in near + outer:
            inside = (at_frame >= 0) & (at_frame < frames) & (at_block >= 0) & (at_block < total_blocks)
            name = jnp.where(inside, at_frame * total_blocks + at_block, -1)
            live = listed[0] == name
            for entry in listed[1:]:
                live = live | (entry == name)
            dead.append(jnp.where(live, 0.0, DEAD))
    return dead


def attend(kept, list_ref, count_ref, gate_ref, q_ref, k_ref, v_ref, own_cross_ref, own_chip_ref,
           odd_edge_ref, even_edge_ref, odd_inner_ref, even_inner_ref, cross_ref, chip_ref, out_ref):
    heads = out_ref.shape[-1] // HD
    block_len = q_ref.shape[1]
    net = lax.axis_index("net")
    base = (net if kept else 1 - net) * out_ref.shape[-1]
    near = ((even_edge_ref, even_inner_ref), (odd_edge_ref, odd_inner_ref))
    dead = dead_rows(list_ref, count_ref, block_len)

    def at_head(head):
        return slice(head * HD, (head + 1) * HD), pl.ds(pl.multiple_of(base + head * HD, HD), HD)

    def rows(head, side, own_ref):
        here, there = at_head(head)
        parts = [own_ref[0, :, there], own_ref[1, :, there],
                 own_cross_ref[side, :, there], own_chip_ref[side, :, there]]
        for at, (edge_ref, inner_ref) in enumerate(near):
            parts += [edge_ref[side, :, here], inner_ref[side, :, here],
                      cross_ref[at, side, :, here], chip_ref[at, side, :, here]]
        return jnp.concatenate(parts, axis=0)

    def score(head):
        _, there = at_head(head)
        queries = jnp.concatenate([q_ref[0, :, there], q_ref[1, :, there]], axis=0)
        return lax.dot_general(
            rows(head, 0, k_ref), queries, (((1,), (1,)), ((), ())), preferred_element_type=jnp.float32
        )

    scores = score(0)
    for head in range(heads):
        here, there = at_head(head)
        later = score(head + 1) if head + 1 < heads else None
        scores = scores * (HD ** (-0.5) * LOG2E)
        scores = jnp.concatenate(
            [scores[at * block_len:(at + 1) * block_len] + row for at, row in enumerate(dead)], axis=0
        )
        expo = jnp.exp2(scores - jnp.max(scores, axis=0, keepdims=True))
        total = jnp.sum(expo, axis=0, keepdims=True)
        mixed = lax.dot_general(
            expo.astype(jnp.bfloat16), rows(head, 1, v_ref), (((0,), (0,)), ((), ())),
            preferred_element_type=jnp.float32,
        )
        total = jnp.transpose(jnp.broadcast_to(total, (8, 2 * block_len)))[:, 0:1]
        mixed = mixed / total * gate_ref[0:1, there]
        out_ref[0, :, here] = mixed[:block_len].astype(out_ref.dtype)
        out_ref[1, :, here] = mixed[block_len:].astype(out_ref.dtype)
        scores = later


def attention(kept, listed, count, operands, width, dtype):
    queries = operands[1]
    blocks, block_len, _ = queries.shape
    keys_seen = 12 * block_len
    vmem, smem = (pl.BlockSpec(memory_space=space) for space in (pltpu.VMEM, pltpu.SMEM))
    return kernel_call(
        functools.partial(attend, kept), [smem, smem] + [vmem] * len(operands),
        jax.ShapeDtypeStruct((blocks, block_len, width), dtype),
        (listed, count, *on_chip(*operands)),
        cost_estimate=pl.CostEstimate(
            flops=4 * blocks * block_len * keys_seen * width,
            bytes_accessed=4 * keys_seen * width,
            transcendentals=blocks * block_len * keys_seen * width // HD,
        ),
        compiler_params=pltpu.CompilerParams(vmem_limit_bytes=VMEM_LIMIT),
    )


def shards(query_rows, key_rows, value_rows, time_proj, block_list, block_count, timestep):
    queries, keys, values = query_rows[0, 0], key_rows[0, 0], value_rows[0, 0]
    blocks_here, _, features = queries.shape
    assert query_rows.shape[1] == 1 and blocks_here == 2
    width = features // lax.axis_size("net")
    time_pairs = (swaps(lax.axis_size("tm"), 1), swaps(lax.axis_size("tm"), 0))
    chip_pairs, cross_pairs = (swaps(lax.axis_size("space"), first) for first in (0, 1))

    edge_away, inner_away = pack(keys, values, [("edge", "away"), ("inner", "away")])
    first_edge = [lax.ppermute(edge_away, "tm", pairs) for pairs in time_pairs]
    first_inner = [lax.ppermute(inner_away, "tm", pairs) for pairs in time_pairs]
    edge_own, inner_own, edge_kept, inner_kept, gate = pack(
        keys, values, [("edge", "both"), ("inner", "both"), ("edge", "kept"), ("inner", "kept")],
        time_feature(timestep), time_proj[0],
    )
    own_cross = lax.ppermute(edge_own, "space", cross_pairs)
    own_chip = lax.ppermute(inner_own, "space", chip_pairs)
    kept_edge = [lax.ppermute(edge_kept, "tm", pairs) for pairs in time_pairs]
    kept_inner = [lax.ppermute(inner_kept, "tm", pairs) for pairs in time_pairs]

    listed = (block_list[0], block_count)
    shared = (gate, queries, keys, values, own_cross, own_chip)

    first_cross = lax.ppermute(join(*first_edge), "space", cross_pairs)
    first_chip = lax.ppermute(join(*first_inner), "space", chip_pairs)
    sent = attention(
        False, *listed, (*shared, *first_edge, *first_inner, first_cross, first_chip),
        width, jnp.bfloat16,
    )
    arrived = lax.ppermute(sent, "net", swaps(lax.axis_size("net"), 0))
    kept_cross = lax.ppermute(join(*kept_edge), "space", cross_pairs)
    kept_chip = lax.ppermute(join(*kept_inner), "space", chip_pairs)
    here = attention(
        True, *listed, (*shared, *kept_edge, *kept_inner, kept_cross, kept_chip),
        width, jnp.float32,
    )
    return (here + arrived).astype(jnp.bfloat16)[None]


def solution(mesh):
    return jax.shard_map(
        shards,
        mesh=mesh,
        in_specs=(
            P("net", "tm", "space", None, None),
            P("net", "tm", "space", None, None),
            P("net", "tm", "space", None, None),
            P("net", None, None),
            P("tm", "space", None),
            P("tm", "space"),
            P(),
        ),
        out_specs=P("tm", "space", None, "net"),
        check_vma=False,
    )
```
